32 devices in a mesh: groups: 2 (over x), ctx: 16 (over z, y, core).
Axes of the slice: x: 2, y: 2, z: 4, core: 2. Of those that a mesh axis runs over, the one named last changes fastest.
Arguments:
- queries: bfloat16 [8192, 1024], P(('groups', 'ctx')), parts along dimension 0, may hold values from -128 to 128
- keys: bfloat16 [8192, 128], P(('groups', 'ctx')), parts along dimension 0, may hold values from -32 to 32
- values: bfloat16 [8192, 128], P(('groups', 'ctx')), parts along dimension 0, may hold values from -6 to 6
- doc_ids: int32 [8192], P(('groups', 'ctx')), parts along dimension 0, may hold values from 0 to 2, never falling along the last dimension, each value on 1 to 3072 neighbouring positions
Outputs:
- attended: bfloat16 [8192, 1024], P(('groups', 'ctx')), parts along dimension 0
The draws below stay inside these ranges and needn't reach their ends.
There are 2 independent parts, one for each index of `groups`. The reference program is written for one: setup_inputs(seed, part) draws one part's arguments, and reference() takes and returns one part's arrays. A program takes and returns all parts, laid end to end along the dimension named above; each array names one. Nothing has to cross between parts.
All inputs are finite; a program needn't handle non-finite values.
Results may differ from the reference program's by a relative error of at most 0.0041.
Values may be sent and summed in bfloat16 or wider, within the bound.
A program may use at most 64 MiB of HBM per device.

```python
import math
import jax
import jax.numpy as jnp
import numpy as np
from jax import lax

HEADS = 8
HEAD_DIM = 128
DOCS = 3
HALF = 128
SEQ = 4096
LONGEST = 3072


def drawn_pair(key):
    base = jax.random.fold_in(key, 7)
    key_one, key_two = jax.random.split(base, 2)
    keys = jnp.clip(jax.random.normal(key_one, (SEQ, HEAD_DIM), jnp.float32), -6.0, 6.0)
    queries = jnp.clip(jax.random.normal(key_two, (SEQ, HEADS * HEAD_DIM), jnp.float32), -6.0, 6.0)
    return (queries, keys)


def draw_queries(key, part):
    return drawn_pair(key)[0].astype(jnp.bfloat16)


def draw_keys(key, part):
    return drawn_pair(key)[1].astype(jnp.bfloat16)


def level_of(stream_key, dims, cuts, smallest, top_value):
    gain = 1.0
    for dim, parts in cuts:
        heights = jax.random.uniform(jax.random.fold_in(jax.random.fold_in(stream_key, 6), dim), (parts,), jnp.float32, smallest / len(cuts), top_value / len(cuts))
        gain = gain * jnp.repeat(jnp.exp(heights), dims[dim] // parts).reshape((-1,) + (1,) * (len(dims) - 1 - dim))
    return gain


def profile(number_of, total, limit, lean):
    portions = [(1 << 20) // math.isqrt(grade ** lean) + 1 for grade in range(2, number_of + 1)]
    rest, counts = total - limit - (number_of - 1), [1] * (number_of - 1)
    while rest > 0:
        candidates = [i for i in range(number_of - 1) if counts[i] < limit]
        pool, left = sum([portions[i] for i in candidates]), rest
        for i in candidates:
            extra = min(limit - counts[i], max(1, left * portions[i] // pool), rest)
            counts[i] = counts[i] + extra
            rest = rest - extra
    return np.array([limit] + counts)


def ragged_sizes(rng, amount, total, bound, lean):
    if amount == 2:
        one = jax.random.randint(rng, (), max(1, total - bound), min(bound, total - 1) + 1)
        return jnp.stack([one, total - one])
    sizes = jnp.asarray(profile(amount, total, bound, lean), jnp.int32)
    couples = (amount - 1) // 2
    giver, receiver = sizes[1:1 + 2 * couples:2], sizes[2:2 + 2 * couples:2]
    slack = jnp.minimum(giver - 1, bound - receiver)
    passed = jax.random.randint(jax.random.fold_in(rng, 1), (couples,), 0, 1 << 20) % (slack + 1)
    sizes = sizes.at[1:1 + 2 * couples:2].set(giver - passed).at[2:2 + 2 * couples:2].set(receiver + passed)
    return sizes[jax.random.permutation(jax.random.fold_in(rng, 2), amount)]


def centred(key, dims, deviation, reach, cuts=(), kind=jnp.bfloat16):
    values = deviation * jax.random.normal(key, dims, jnp.float32)
    if cuts:
        values = values * level_of(key, dims, cuts, -0.22, 0.18)
    return jnp.clip(values, -reach, reach).astype(kind)


def setup_inputs(seed: int = 0, part: int = 0) -> dict:
    splits = jax.random.split(jax.random.key(seed), 5)
    part_splits = jax.random.split(jax.random.fold_in(splits[4], part), 5)
    return {
        "queries": draw_queries(jax.random.fold_in(jax.random.fold_in(splits[4], part), 71), part),
        "keys": draw_keys(jax.random.fold_in(jax.random.fold_in(splits[4], part), 71), part),
        "values": centred(part_splits[2], (SEQ, HEAD_DIM), 1.0, 6.0, ((0, 16),)),
        "doc_ids": jnp.searchsorted(jnp.cumsum(ragged_sizes(part_splits[3], DOCS, SEQ, LONGEST, 0)), jnp.arange(SEQ), side="right").astype(jnp.int32),
    }


def reference(queries, keys, values, doc_ids):
    score_scale = HEAD_DIM ** -0.5
    positions = jnp.arange(SEQ, dtype=jnp.int32)

    def query_block(block_index):
        start_row = (block_index * HALF).astype(jnp.int32)
        query_rows = lax.dynamic_slice_in_dim(queries, start_row, HALF, 0).reshape(HALF * HEADS, HEAD_DIM)
        scores = jnp.dot(query_rows, keys.T, preferred_element_type=jnp.float32) * score_scale
        query_place = jnp.repeat(start_row + jnp.arange(HALF, dtype=jnp.int32), HEADS)
        query_doc = jnp.repeat(lax.dynamic_slice_in_dim(doc_ids, start_row, HALF, 0), HEADS)
        visible = (positions[None, :] <= query_place[:, None]) & (doc_ids[None, :] == query_doc[:, None])
        row_max = jnp.max(jnp.where(visible, scores, -jnp.inf), axis=1)
        weights = jnp.where(visible, jnp.exp(scores - row_max[:, None]), 0.0)
        row_sum = jnp.sum(weights, axis=1)
        result = jnp.dot(weights.astype(jnp.bfloat16), values, preferred_element_type=jnp.float32) / row_sum[:, None]
        return result.astype(jnp.bfloat16).reshape(HALF, HEADS * HEAD_DIM)

    blocks = lax.map(query_block, jnp.arange(SEQ // HALF, dtype=jnp.int32))
    return blocks.reshape(SEQ, HEADS * HEAD_DIM)
```

```python
import functools

import jax
import jax.numpy as jnp
from jax import lax
from jax.experimental import pallas as pl
from jax.experimental.pallas import tpu as pltpu
from jax.sharding import PartitionSpec as P

HIDDEN = -1e30
LOG2E = 1.4426950408889634


def kernel(
    n,
    q_ref,
    k_hbm,
    v_hbm,
    d_hbm,
    o_ref,
    kv,
    docs,
    bias,
    m_ref,
    l_ref,
    acc_ref,
    fill_sem,
    send_kv,
    send_doc,
    recv_kv,
    recv_doc,
):
    rows, width = q_ref.shape
    dim = k_hbm.shape[1]
    heads = width // dim
    levels = n // 4
    window = 3 * n // 4
    me = lax.axis_index("ctx")
    z = me // 4
    r = me % 4
    y = r // 2
    c = r % 2
    up = me + 4
    across = z * 4 + (1 - y) * 2 + c
    partner = z * 4 + y * 2 + (1 - c)
    scale = dim ** (-0.5) * LOG2E

    def span(block):
        return pl.ds(pl.multiple_of(block * rows, rows), rows)

    fills = [
        pltpu.make_async_copy(k_hbm, kv.at[0, span(me), :], fill_sem.at[0]),
        pltpu.make_async_copy(v_hbm, kv.at[1, span(me), :], fill_sem.at[1]),
        pltpu.make_async_copy(d_hbm, docs.at[me], fill_sem.at[2]),
    ]
    for fill in fills:
        fill.start()

    barrier = pltpu.get_barrier_semaphore()

    def greet(device):
        pl.semaphore_signal(
            barrier, inc=1, device_id={"ctx": device}, device_id_type=pl.DeviceIdType.MESH
        )

    greet(partner)
    greet(across)

    @pl.when(z > 0)
    def _():
        greet(me - 4)

    @pl.when(z < levels - 1)
    def _():
        greet(up)

    pl.semaphore_wait(barrier, 2 + jnp.minimum(z, 1) + jnp.minimum(levels - 1 - z, 1))

    for fill in fills:
        fill.wait()

    def copies(stream, slot, block, device):
        return (
            pltpu.make_async_remote_copy(
                src_ref=kv.at[:, span(block), :],
                dst_ref=kv.at[:, span(block), :],
                send_sem=send_kv.at[stream, slot],
                recv_sem=recv_kv.at[stream, slot],
                device_id={"ctx": device},
                device_id_type=pl.DeviceIdType.MESH,
            ),
            pltpu.make_async_remote_copy(
                src_ref=docs.at[block],
                dst_ref=docs.at[block],
                send_sem=send_doc.at[stream, slot],
                recv_sem=recv_doc.at[stream, slot],
                device_id={"ctx": device},
                device_id_type=pl.DeviceIdType.MESH,
            ),
        )

    def start(stream, slot, block, device):
        for copy in copies(stream, slot, block, device):
            copy.start()

    def arrived(stream, slot, block, device):
        for copy in copies(stream, slot, block, device):
            copy.wait_recv()

    def sent(stream, slot, block, device):
        for copy in copies(stream, slot, block, device):
            copy.wait_send()

    def relay(level):
        block = level * 4 + r

        @pl.when(z < levels - 1)
        def _():
            start(0, level, block, up)

        start(1, level, block, across)
        start(2, level, block, partner)

    m_ref[...] = jnp.full_like(m_ref, HIDDEN)
    l_ref[...] = jnp.zeros_like(l_ref)
    acc_ref[...] = jnp.zeros_like(acc_ref)
    doc_col = jnp.broadcast_to(docs[me], (dim, rows)).T
    relay(z)

    def process(chunk):
        @pl.when((chunk <= me // 2) & (chunk * 2 + 1 >= me - window))
        def _():
            row_id = me * rows + lax.broadcasted_iota(jnp.int32, (rows, dim), 0)
            lane = lax.broadcasted_iota(jnp.int32, (rows, dim), 1)
            for half in range(2):
                doc_row = docs[chunk * 2 + half]
                for part in range(rows // dim):
                    key_id = (chunk * 2 + half) * rows + part * dim + lane
                    same = doc_row[:, part * dim : (part + 1) * dim] == doc_col
                    bias[:, pl.ds(half * rows + part * dim, dim)] = jnp.where(
                        same & (key_id <= row_id), 0.0, HIDDEN
                    )
            place = pl.ds(pl.multiple_of(chunk * 2 * rows, 2 * rows), 2 * rows)
            for head in range(heads):
                cols = slice(head * dim, (head + 1) * dim)
                s = (
                    lax.dot_general(
                        q_ref[:, cols],
                        kv[0, place, :],
                        (((1,), (1,)), ((), ())),
                        preferred_element_type=jnp.float32,
                    )
                    + bias[...]
                )
                old = m_ref[head]
                new = jnp.maximum(old, jnp.max(s, axis=1, keepdims=True))
                m_ref[head] = new
                factor = jnp.exp2((old - new) * scale)
                w = jnp.exp2((s - jnp.tile(new, (1, 2 * rows // dim))) * scale)
                l_ref[head] = l_ref[head] * factor + jnp.sum(w, axis=1, keepdims=True)
                acc_ref[head] = acc_ref[head] * factor + jnp.dot(
                    w.astype(jnp.bfloat16), kv[1, place, :], preferred_element_type=jnp.float32
                )

    def step(i, carry):
        level = z - i
        arrived(2, level, level * 4 + 2 * y + 1 - c, partner)
        process(level * 2 + y)

        @pl.when(level > 0)
        def _():
            arrived(0, level - 1, (level - 1) * 4 + r, up)
            relay(level - 1)

        other = level * 4 + 2 * (1 - y) + c
        arrived(1, level, other, across)
        start(3, level, other, partner)

        @pl.when(i > 0)
        def _():
            arrived(3, level + 1, (level + 1) * 4 + 2 * (1 - y) + 1 - c, partner)
            process((level + 1) * 2 + 1 - y)

        return carry

    lax.fori_loop(0, z + 1, step, 0)
    arrived(3, 0, 2 * (1 - y) + 1 - c, partner)
    process(1 - y)

    for head in range(heads):
        o_ref[:, head * dim : (head + 1) * dim] = (acc_ref[head] / l_ref[head]).astype(o_ref.dtype)

    def finish(level, carry):
        block = level * 4 + r

        @pl.when(z < levels - 1)
        def _():
            sent(0, level, block, up)

        sent(1, level, block, across)
        sent(2, level, block, partner)
        sent(3, level, level * 4 + 2 * (1 - y) + c, partner)
        return carry

    lax.fori_loop(0, z + 1, finish, 0)


def solution(mesh):
    n = mesh.shape["ctx"]

    def on_device(queries, keys, values, doc_ids):
        rows, width = queries.shape
        dim = keys.shape[1]
        heads = width // dim
        levels = n // 4
        vmem = pl.BlockSpec(memory_space=pltpu.VMEM)
        anywhere = pl.BlockSpec(memory_space=pl.ANY)
        sems = pltpu.SemaphoreType.DMA((4, levels))
        return pl.pallas_call(
            functools.partial(kernel, n),
            out_shape=jax.ShapeDtypeStruct((rows, width), jnp.bfloat16),
            in_specs=[vmem, anywhere, anywhere, anywhere],
            out_specs=vmem,
            scratch_shapes=[
                pltpu.VMEM((2, n * rows, dim), jnp.bfloat16),
                pltpu.VMEM((n, 1, rows), jnp.int32),
                pltpu.VMEM((rows, 2 * rows), jnp.float32),
                pltpu.VMEM((heads, rows, dim), jnp.float32),
                pltpu.VMEM((heads, rows, dim), jnp.float32),
                pltpu.VMEM((heads, rows, dim), jnp.float32),
                pltpu.SemaphoreType.DMA((3,)),
                sems,
                sems,
                sems,
                sems,
            ],
            compiler_params=pltpu.CompilerParams(collective_id=0, has_side_effects=True),
        )(queries, keys, values, doc_ids.reshape(1, rows))

    spec = P(("groups", "ctx"), None)
    return jax.shard_map(
        on_device,
        mesh=mesh,
        in_specs=(spec, spec, spec, P(("groups", "ctx"))),
        out_specs=spec,
        check_vma=False,
    )
```

```python
import functools

import jax
import jax.numpy as jnp
from jax import lax
from jax.experimental import pallas as pl
from jax.experimental.pallas import tpu as pltpu
from jax.sharding import PartitionSpec as P

HIDDEN = -1e30
LOG2E = 1.4426950408889634
TILE_HEADS = 2


def kernel(
    n,
    q_hbm,
    k_hbm,
    v_hbm,
    d_hbm,
    o_hbm,
    q_ref,
    o_ref,
    kv,
    docs,
    bias,
    m_ref,
    acc_ref,
    qs,
    fill_sem,
    out_sem,
    send_kv,
    recv_kv,
    send_doc,
    recv_doc,
):
    rows, width = q_hbm.shape
    dim = k_hbm.shape[1]
    heads = width // dim
    levels = n // 4
    window = 3 * n // 4
    depth = (window + 3) // 4
    me = lax.axis_index("ctx")
    z = me // 4
    r = me % 4
    y = r // 2
    c = r % 2
    chip = me // 2
    up = me + 4
    across = z * 4 + (1 - y) * 2 + c
    partner = z * 4 + y * 2 + (1 - c)
    scale = dim ** (-0.5) * LOG2E
    keys_wide = 2 * rows

    def span(block):
        return pl.ds(pl.multiple_of(block * rows, rows), rows)

    fills = [
        pltpu.make_async_copy(k_hbm, kv.at[0, span(me), :], fill_sem.at[0]),
        pltpu.make_async_copy(v_hbm, kv.at[1, span(me), :], fill_sem.at[1]),
        pltpu.make_async_copy(d_hbm, docs.at[me], fill_sem.at[2]),
    ]
    for fill in fills:
        fill.start()
    query_fill = pltpu.make_async_copy(q_hbm, q_ref, fill_sem.at[3])
    query_fill.start()

    barrier = pltpu.get_barrier_semaphore()

    def greet(device):
        pl.semaphore_signal(
            barrier, inc=1, device_id={"ctx": device}, device_id_type=pl.DeviceIdType.MESH
        )

    greet(partner)
    greet(across)

    @pl.when(z > 0)
    def _():
        greet(me - 4)

    @pl.when(z < levels - 1)
    def _():
        greet(up)

    pl.semaphore_wait(barrier, 2 + jnp.minimum(z, 1) + jnp.minimum(levels - 1 - z, 1))

    def copies(stream, level, piece, block, device):
        made = [
            pltpu.make_async_remote_copy(
                src_ref=kv.at[piece, span(block), :],
                dst_ref=kv.at[piece, span(block), :],
                send_sem=send_kv.at[stream, level, piece],
                recv_sem=recv_kv.at[stream, level, piece],
                device_id={"ctx": device},
                device_id_type=pl.DeviceIdType.MESH,
            )
        ]
        if piece == 0:
            made.append(
                pltpu.make_async_remote_copy(
                    src_ref=docs.at[block],
                    dst_ref=docs.at[block],
                    send_sem=send_doc.at[stream, level],
                    recv_sem=recv_doc.at[stream, level],
                    device_id={"ctx": device},
                    device_id_type=pl.DeviceIdType.MESH,
                )
            )
        return made

    def start(*where):
        for copy in copies(*where):
            copy.start()

    def arrived(*where):
        for copy in copies(*where):
            copy.wait_recv()

    def sent(*where):
        for copy in copies(*where):
            copy.wait_send()

    def needs(some_chip, chunk):
        return (chunk <= some_chip) & (2 * chunk + 1 >= 2 * some_chip - window)

    def climbs(level):
        return (z < levels - 1) & (z - level < depth)

    def crosses(level):
        return needs(2 * z + 1 - y, 2 * level + y)

    def crossed(level):
        return needs(chip, 2 * level + 1 - y)

    def relay(level, piece):
        block = level * 4 + r

        @pl.when(climbs(level))
        def _():
            start(0, level, piece, block, up)

        @pl.when(crosses(level))
        def _():
            start(1, level, piece, block, across)

        start(2, level, piece, block, partner)

    for fill in fills[:1] + fills[2:]:
        fill.wait()
    relay(z, 0)
    fills[1].wait()
    relay(z, 1)

    lane = lax.broadcasted_iota(jnp.int32, (rows, dim), 1)
    row_id = me * rows + lax.broadcasted_iota(jnp.int32, (rows, dim), 0)
    doc_col = jnp.broadcast_to(docs[me], (dim, rows)).T
    query_marks = jnp.where(lane == doc_col, 0.0, HIDDEN).astype(jnp.bfloat16)
    query_fill.wait()
    for head in range(heads):
        here = slice(head * rows, (head + 1) * rows)
        qs[here, :dim] = q_ref[:, head * dim : (head + 1) * dim]
        qs[here, dim:] = query_marks

    def attend(chunk, first, hooks):
        place = pl.ds(pl.multiple_of(chunk * keys_wide, keys_wide), keys_wide)
        marks = []
        for half in range(2):
            key_col = jnp.broadcast_to(docs[chunk * 2 + half], (dim, rows)).T
            marks.append(jnp.where(lane == key_col, 1.0, 0.0).astype(jnp.bfloat16))
        k_chunk = jnp.concatenate([kv[0, place, :], jnp.concatenate(marks, axis=0)], axis=1)
        v_chunk = jnp.concatenate(
            [kv[1, place, :], jnp.ones((keys_wide, dim), jnp.bfloat16)], axis=1
        )
        if first:
            for part in range(keys_wide // dim):
                key_id = chunk * keys_wide + part * dim + lane
                bias[:, part * dim : (part + 1) * dim] = jnp.where(key_id <= row_id, 0.0, HIDDEN)
        tile_rows = TILE_HEADS * rows

        def scores(tile):
            return lax.dot_general(
                qs[tile * tile_rows : (tile + 1) * tile_rows, :],
                k_chunk,
                (((1,), (1,)), ((), ())),
                preferred_element_type=jnp.float32,
            )

        tiles = heads // TILE_HEADS
        following = scores(0)
        for tile in range(tiles):
            s = following
            if tile + 1 < tiles:
                following = scores(tile + 1)
            here = slice(tile * tile_rows, (tile + 1) * tile_rows)
            if first:
                s = s + jnp.concatenate([bias[...]] * TILE_HEADS, axis=0)
            new = jnp.max(s, axis=1, keepdims=True)
            if first:
                new = jnp.broadcast_to(new, (tile_rows, dim))
            else:
                old = m_ref[here]
                new = jnp.maximum(old, new)
            m_ref[here] = new
            w = jnp.exp2((s - jnp.tile(new, (1, keys_wide // dim))) * scale)
            part = jnp.dot(w.astype(jnp.bfloat16), v_chunk, preferred_element_type=jnp.float32)
            if first:
                acc_ref[here] = part
            else:
                acc_ref[here] = (
                    acc_ref[here] * jnp.tile(jnp.exp2((old - new) * scale), (1, 2)) + part
                )
            if tile < len(hooks):
                hooks[tile]()

    def process(chunk, hooks=()):
        needed = (chunk <= chip) & (chunk * 2 + 1 >= me - window)

        @pl.when(needed)
        def _():
            attend(chunk, False, hooks)

        if hooks:

            @pl.when(jnp.logical_not(needed))
            def _():
                for hook in hooks:
                    hook()

    def from_below(level, piece):
        def hook():
            @pl.when(level > jnp.maximum(z - depth, 0))
            def _():
                arrived(0, level - 1, piece, (level - 1) * 4 + r, up)
                relay(level - 1, piece)

        return hook

    def from_across(level, piece):
        block = level * 4 + 2 * (1 - y) + c

        def hook():
            @pl.when(crossed(level))
            def _():
                arrived(1, level, piece, block, across)
                start(3, level, piece, block, partner)

        return hook

    def own_column(level):
        for piece in range(2):
            arrived(2, level, piece, level * 4 + 2 * y + 1 - c, partner)

    def other_column(level):
        @pl.when(crossed(level))
        def _():
            for piece in range(2):
                arrived(3, level, piece, level * 4 + 2 * (1 - y) + 1 - c, partner)

    def hooks_of(level):
        return (
            from_below(level, 0),
            from_across(level, 0),
            from_below(level, 1),
            from_across(level, 1),
        )

    own_column(z)
    attend(chip, True, hooks_of(z))

    def step(i, carry):
        level = z - i
        own_column(level)
        process(level * 2 + y, hooks_of(level))
        other_column(level + 1)
        process((level + 1) * 2 + 1 - y)
        return carry

    last = jnp.minimum(z, depth)
    lax.fori_loop(1, last + 1, step, 0)
    other_column(z - last)
    process((z - last) * 2 + 1 - y)

    def out_copy(head):
        cols = slice(head * dim, (head + 1) * dim)
        return pltpu.make_async_copy(o_ref.at[:, cols], o_hbm.at[:, cols], out_sem.at[head])

    for head in range(heads):
        here = slice(head * rows, (head + 1) * rows)
        o_ref[:, head * dim : (head + 1) * dim] = (acc_ref[here, :dim] / acc_ref[here, dim:]).astype(
            o_ref.dtype
        )
        out_copy(head).start()

    def finish(i, carry):
        level = z - i
        block = level * 4 + r
        for piece in range(2):

            @pl.when(climbs(level))
            def _():
                sent(0, level, piece, block, up)

            @pl.when(crosses(level))
            def _():
                sent(1, level, piece, block, across)

            sent(2, level, piece, block, partner)

            @pl.when(crossed(level))
            def _():
                sent(3, level, piece, level * 4 + 2 * (1 - y) + c, partner)

        return carry

    lax.fori_loop(0, last + 1, finish, 0)
    for head in range(heads):
        out_copy(head).wait()


def solution(mesh):
    n = mesh.shape["ctx"]

    def on_device(queries, keys, values, doc_ids):
        rows, width = queries.shape
        dim = keys.shape[1]
        heads = width // dim
        levels = n // 4
        anywhere = pl.BlockSpec(memory_space=pl.ANY)
        piece_sems = pltpu.SemaphoreType.DMA((4, levels, 2))
        doc_sems = pltpu.SemaphoreType.DMA((4, levels))
        return pl.pallas_call(
            functools.partial(kernel, n),
            out_shape=jax.ShapeDtypeStruct((rows, width), jnp.bfloat16),
            in_specs=[anywhere] * 4,
            out_specs=anywhere,
            scratch_shapes=[
                pltpu.VMEM((rows, width), jnp.bfloat16),
                pltpu.VMEM((rows, width), jnp.bfloat16),
                pltpu.VMEM((2, n * rows, dim), jnp.bfloat16),
                pltpu.VMEM((n, 1, rows), jnp.int32),
                pltpu.VMEM((rows, 2 * rows), jnp.float32),
                pltpu.VMEM((heads * rows, dim), jnp.float32),
                pltpu.VMEM((heads * rows, 2 * dim), jnp.float32),
                pltpu.VMEM((heads * rows, 2 * dim), jnp.bfloat16),
                pltpu.SemaphoreType.DMA((4,)),
                pltpu.SemaphoreType.DMA((heads,)),
                piece_sems,
                piece_sems,
                doc_sems,
                doc_sems,
            ],
            compiler_params=pltpu.CompilerParams(collective_id=0, has_side_effects=True),
        )(queries, keys, values, doc_ids.reshape(1, rows))

    spec = P(("groups", "ctx"), None)
    return jax.shard_map(
        on_device,
        mesh=mesh,
        in_specs=(spec, spec, spec, P(("groups", "ctx"))),
        out_specs=spec,
        check_vma=False,
    )
```

```python
import functools

import jax
import jax.numpy as jnp
from jax import lax
from jax.experimental import pallas as pl
from jax.experimental.pallas import tpu as pltpu
from jax.sharding import PartitionSpec as P

HIDDEN = -1e30
LOG2E = 1.4426950408889634
TILE_HEADS = 2


def kernel(
    n,
    q_hbm,
    k_hbm,
    v_hbm,
    d_hbm,
    o_hbm,
    q_ref,
    o_ref,
    kv,
    docs,
    bias,
    m_ref,
    acc_ref,
    qs,
    fill_sem,
    out_sem,
    send_kv,
    recv_kv,
    send_doc,
    recv_doc,
):
    rows, width = q_hbm.shape
    dim = k_hbm.shape[1]
    heads = width // dim
    levels = n // 4
    window = 3 * n // 4
    depth = (window + 3) // 4
    me = lax.axis_index("ctx")
    z = me // 4
    r = me % 4
    y = r // 2
    c = r % 2
    chip = me // 2
    up = me + 4
    across = z * 4 + (1 - y) * 2 + c
    partner = z * 4 + y * 2 + (1 - c)
    scale = dim ** (-0.5) * LOG2E
    keys_wide = 2 * rows

    def span(block):
        return pl.ds(pl.multiple_of(block * rows, rows), rows)

    fills = [
        pltpu.make_async_copy(k_hbm, kv.at[0, span(me), :], fill_sem.at[0]),
        pltpu.make_async_copy(v_hbm, kv.at[1, span(me), :], fill_sem.at[1]),
        pltpu.make_async_copy(d_hbm, docs.at[me], fill_sem.at[2]),
    ]
    for fill in fills:
        fill.start()
    query_fill = pltpu.make_async_copy(q_hbm, q_ref, fill_sem.at[3])
    query_fill.start()

    barrier = pltpu.get_barrier_semaphore()

    def greet(device):
        pl.semaphore_signal(
            barrier, inc=1, device_id={"ctx": device}, device_id_type=pl.DeviceIdType.MESH
        )

    greet(partner)
    greet(across)

    @pl.when(z > 0)
    def _():
        greet(me - 4)

    @pl.when(z < levels - 1)
    def _():
        greet(up)

    pl.semaphore_wait(barrier, 2 + jnp.minimum(z, 1) + jnp.minimum(levels - 1 - z, 1))

    def copies(stream, level, piece, block, device):
        made = [
            pltpu.make_async_remote_copy(
                src_ref=kv.at[piece, span(block), :],
                dst_ref=kv.at[piece, span(block), :],
                send_sem=send_kv.at[stream, level, piece],
                recv_sem=recv_kv.at[stream, level, piece],
                device_id={"ctx": device},
                device_id_type=pl.DeviceIdType.MESH,
            )
        ]
        if piece == 0:
            made.append(
                pltpu.make_async_remote_copy(
                    src_ref=docs.at[block],
                    dst_ref=docs.at[block],
                    send_sem=send_doc.at[stream, level],
                    recv_sem=recv_doc.at[stream, level],
                    device_id={"ctx": device},
                    device_id_type=pl.DeviceIdType.MESH,
                )
            )
        return made

    def start(*where):
        for copy in copies(*where):
            copy.start()

    def arrived(*where):
        for copy in copies(*where):
            copy.wait_recv()

    def sent(*where):
        for copy in copies(*where):
            copy.wait_send()

    def needs(some_chip, chunk):
        return (chunk <= some_chip) & (2 * chunk + 1 >= 2 * some_chip - window)

    def climbs(level):
        return (z < levels - 1) & (z - level < depth)

    def crosses(level):
        return needs(2 * z + 1 - y, 2 * level + y)

    def crossed(level):
        return needs(chip, 2 * level + 1 - y)

    def relay(level, piece):
        block = level * 4 + r

        @pl.when(climbs(level))
        def _():
            start(0, level, piece, block, up)

        @pl.when(crosses(level))
        def _():
            start(1, level, piece, block, across)

        start(2, level, piece, block, partner)

    for fill in fills[:1] + fills[2:]:
        fill.wait()
    relay(z, 0)
    fills[1].wait()
    relay(z, 1)

    lane = lax.broadcasted_iota(jnp.int32, (rows, dim), 1)
    row_id = me * rows + lax.broadcasted_iota(jnp.int32, (rows, dim), 0)
    doc_col = jnp.broadcast_to(docs[me], (dim, rows)).T
    query_marks = jnp.where(lane == doc_col, 0.0, HIDDEN).astype(jnp.bfloat16)
    query_fill.wait()
    for head in range(heads):
        here = slice(head * rows, (head + 1) * rows)
        qs[here, :dim] = q_ref[:, head * dim : (head + 1) * dim]
        qs[here, dim:] = query_marks

    def attend(chunk, first, hooks):
        place = pl.ds(pl.multiple_of(chunk * keys_wide, keys_wide), keys_wide)
        marks = []
        for half in range(2):
            key_col = jnp.broadcast_to(docs[chunk * 2 + half], (dim, rows)).T
            marks.append(jnp.where(lane == key_col, 1.0, 0.0).astype(jnp.bfloat16))
        k_chunk = jnp.concatenate([kv[0, place, :], jnp.concatenate(marks, axis=0)], axis=1)
        v_chunk = jnp.concatenate(
            [kv[1, place, :], jnp.ones((keys_wide, dim), jnp.bfloat16)], axis=1
        )
        if first:
            for part in range(keys_wide // dim):
                key_id = chunk * keys_wide + part * dim + lane
                bias[:, part * dim : (part + 1) * dim] = jnp.where(key_id <= row_id, 0.0, HIDDEN)
        tile_rows = TILE_HEADS * rows

        def scores(tile):
            return lax.dot_general(
                qs[tile * tile_rows : (tile + 1) * tile_rows, :],
                k_chunk,
                (((1,), (1,)), ((), ())),
                preferred_element_type=jnp.float32,
            )

        tiles = heads // TILE_HEADS
        following = scores(0)
        for tile in range(tiles):
            s = following
            if tile + 1 < tiles:
                following = scores(tile + 1)
            here = slice(tile * tile_rows, (tile + 1) * tile_rows)
            if first:
                s = s + jnp.concatenate([bias[...]] * TILE_HEADS, axis=0)
            new = jnp.max(s, axis=1, keepdims=True)
            if first:
                new = jnp.broadcast_to(new, (tile_rows, dim))
            else:
                old = m_ref[here]
                new = jnp.maximum(old, new)
            m_ref[here] = new
            w = jnp.exp2((s - jnp.tile(new, (1, keys_wide // dim))) * scale)
            part = jnp.dot(w.astype(jnp.bfloat16), v_chunk, preferred_element_type=jnp.float32)
            if first:
                acc_ref[here] = part
            else:
                acc_ref[here] = (
                    acc_ref[here] * jnp.tile(jnp.exp2((old - new) * scale), (1, 2)) + part
                )
            if tile < len(hooks):
                hooks[tile]()

    def process(chunk, hooks=()):
        needed = (chunk <= chip) & (chunk * 2 + 1 >= me - window)

        @pl.when(needed)
        def _():
            attend(chunk, False, hooks)

        if hooks:

            @pl.when(jnp.logical_not(needed))
            def _():
                for hook in hooks:
                    hook()

    def from_below(level, piece):
        def hook():
            @pl.when(level > jnp.maximum(z - depth, 0))
            def _():
                arrived(0, level - 1, piece, (level - 1) * 4 + r, up)
                relay(level - 1, piece)

        return hook

    def from_across(level, piece):
        block = level * 4 + 2 * (1 - y) + c

        def hook():
            @pl.when(crossed(level))
            def _():
                arrived(1, level, piece, block, across)
                start(3, level, piece, block, partner)

        return hook

    def own_column(level):
        for piece in range(2):
            arrived(2, level, piece, level * 4 + 2 * y + 1 - c, partner)

    def other_column(level):
        @pl.when(crossed(level))
        def _():
            for piece in range(2):
                arrived(3, level, piece, level * 4 + 2 * (1 - y) + 1 - c, partner)

    def hooks_of(level):
        return (
            from_below(level, 0),
            from_across(level, 0),
            from_below(level, 1),
            from_across(level, 1),
        )

    own_column(z)
    attend(chip, True, hooks_of(z))

    def step(i, carry):
        level = z - i
        own_column(level)
        process(level * 2 + y, hooks_of(level))
        other_column(level + 1)
        process((level + 1) * 2 + 1 - y)
        return carry

    last = jnp.minimum(z, depth)
    lax.fori_loop(1, last + 1, step, 0)
    other_column(z - last)
    process((z - last) * 2 + 1 - y)

    def out_copy(head):
        cols = slice(head * dim, (head + 1) * dim)
        return pltpu.make_async_copy(o_ref.at[:, cols], o_hbm.at[:, cols], out_sem.at[head])

    for head in range(heads):
        here = slice(head * rows, (head + 1) * rows)
        o_ref[:, head * dim : (head + 1) * dim] = (acc_ref[here, :dim] / acc_ref[here, dim:]).astype(
            o_ref.dtype
        )
        out_copy(head).start()

    def finish(i, carry):
        level = z - i
        block = level * 4 + r
        for piece in range(2):

            @pl.when(climbs(level))
            def _():
                sent(0, level, piece, block, up)

            @pl.when(crosses(level))
            def _():
                sent(1, level, piece, block, across)

            sent(2, level, piece, block, partner)

            @pl.when(crossed(level))
            def _():
                sent(3, level, piece, level * 4 + 2 * (1 - y) + c, partner)

        return carry

    lax.fori_loop(0, last + 1, finish, 0)
    for head in range(heads):
        out_copy(head).wait()


def solution(mesh):
    n = mesh.shape["ctx"]

    def on_device(queries, keys, values, doc_ids):
        rows, width = queries.shape
        dim = keys.shape[1]
        heads = width // dim
        levels = n // 4
        anywhere = pl.BlockSpec(memory_space=pl.ANY)
        piece_sems = pltpu.SemaphoreType.DMA((4, levels, 2))
        doc_sems = pltpu.SemaphoreType.DMA((4, levels))
        return pl.pallas_call(
            functools.partial(kernel, n),
            out_shape=jax.ShapeDtypeStruct((rows, width), jnp.bfloat16),
            in_specs=[anywhere] * 4,
            out_specs=anywhere,
            scratch_shapes=[
                pltpu.VMEM((rows, width), jnp.bfloat16),
                pltpu.VMEM((rows, width), jnp.bfloat16),
                pltpu.VMEM((2, n * rows, dim), jnp.bfloat16),
                pltpu.VMEM((n, 1, rows), jnp.int32),
                pltpu.VMEM((rows, 2 * rows), jnp.float32),
                pltpu.VMEM((heads * rows, dim), jnp.float32),
                pltpu.VMEM((heads * rows, 2 * dim), jnp.float32),
                pltpu.VMEM((heads * rows, 2 * dim), jnp.bfloat16),
                pltpu.SemaphoreType.DMA((4,)),
                pltpu.SemaphoreType.DMA((heads,)),
                piece_sems,
                piece_sems,
                doc_sems,
                doc_sems,
            ],
            compiler_params=pltpu.CompilerParams(collective_id=0, has_side_effects=True, vmem_limit_bytes=16 * 1024 * 1024),
        )(*[pltpu.with_memory_space_constraint(a, pltpu.HBM) for a in (queries, keys, values, doc_ids.reshape(1, rows))])

    spec = P(("groups", "ctx"), None)
    return jax.shard_map(
        on_device,
        mesh=mesh,
        in_specs=(spec, spec, spec, P(("groups", "ctx"))),
        out_specs=spec,
        check_vma=False,
    )
```

```python
import functools

import jax
import jax.numpy as jnp
from jax import lax
from jax.experimental import pallas as pl
from jax.experimental.pallas import tpu as pltpu
from jax.sharding import PartitionSpec as P

HIDDEN = -1e30
LOG2E = 1.4426950408889634
TILE_HEADS = 2


def kernel(
    n,
    q_hbm,
    k_hbm,
    v_hbm,
    d_hbm,
    o_hbm,
    q_ref,
    o_ref,
    kv,
    docs,
    bias,
    m_ref,
    acc_ref,
    qs,
    fill_sem,
    out_sem,
    send_kv,
    recv_kv,
    send_doc,
    recv_doc,
):
    rows, width = q_hbm.shape
    dim = k_hbm.shape[1]
    heads = width // dim
    levels = n // 4
    window = 3 * n // 4
    depth = (window + 3) // 4
    me = lax.axis_index("ctx")
    z = me // 4
    r = me % 4
    y = r // 2
    c = r % 2
    chip = me // 2
    up = me + 4
    across = z * 4 + (1 - y) * 2 + c
    partner = z * 4 + y * 2 + (1 - c)
    scale = dim ** (-0.5) * LOG2E
    keys_wide = 2 * rows

    def span(block):
        return pl.ds(pl.multiple_of(block * rows, rows), rows)

    fills = [
        pltpu.make_async_copy(k_hbm, kv.at[0, span(me), :], fill_sem.at[0]),
        pltpu.make_async_copy(v_hbm, kv.at[1, span(me), :], fill_sem.at[1]),
        pltpu.make_async_copy(d_hbm, docs.at[me], fill_sem.at[2]),
    ]
    for fill in fills:
        fill.start()
    query_fill = pltpu.make_async_copy(q_hbm, q_ref, fill_sem.at[3])
    query_fill.start()

    barrier = pltpu.get_barrier_semaphore()

    def greet(device):
        pl.semaphore_signal(
            barrier, inc=1, device_id={"ctx": device}, device_id_type=pl.DeviceIdType.MESH
        )

    greet(partner)
    greet(across)

    @pl.when(z > 0)
    def _():
        greet(me - 4)

    @pl.when(z < levels - 1)
    def _():
        greet(up)

    pl.semaphore_wait(barrier, 2 + jnp.minimum(z, 1) + jnp.minimum(levels - 1 - z, 1))

    def copies(stream, level, piece, block, device):
        made = [
            pltpu.make_async_remote_copy(
                src_ref=kv.at[piece, span(block), :],
                dst_ref=kv.at[piece, span(block), :],
                send_sem=send_kv.at[stream, level, piece],
                recv_sem=recv_kv.at[stream, level, piece],
                device_id={"ctx": device},
                device_id_type=pl.DeviceIdType.MESH,
            )
        ]
        if piece == 0:
            made.append(
                pltpu.make_async_remote_copy(
                    src_ref=docs.at[block],
                    dst_ref=docs.at[block],
                    send_sem=send_doc.at[stream, level],
                    recv_sem=recv_doc.at[stream, level],
                    device_id={"ctx": device},
                    device_id_type=pl.DeviceIdType.MESH,
                )
            )
        return made

    def start(*where):
        for copy in copies(*where):
            copy.start()

    def arrived(*where):
        for copy in copies(*where):
            copy.wait_recv()

    def sent(*where):
        for copy in copies(*where):
            copy.wait_send()

    def needs(some_chip, chunk):
        return (chunk <= some_chip) & (2 * chunk + 1 >= 2 * some_chip - window)

    def climbs(level):
        return (z < levels - 1) & (z - level < depth)

    def crosses(level):
        return needs(2 * z + 1 - y, 2 * level + y)

    def crossed(level):
        return needs(chip, 2 * level + 1 - y)

    def relay(level, piece):
        block = level * 4 + r

        @pl.when(climbs(level))
        def _():
            start(0, level, piece, block, up)

        @pl.when(crosses(level))
        def _():
            start(1, level, piece, block, across)

        start(2, level, piece, block, partner)

    for fill in fills[:1] + fills[2:]:
        fill.wait()
    relay(z, 0)
    fills[1].wait()
    relay(z, 1)

    lane = lax.broadcasted_iota(jnp.int32, (rows, dim), 1)
    row_id = me * rows + lax.broadcasted_iota(jnp.int32, (rows, dim), 0)
    doc_col = jnp.broadcast_to(docs[me], (dim, rows)).T
    query_marks = jnp.where(lane == doc_col, 0.0, HIDDEN).astype(jnp.bfloat16)
    query_fill.wait()
    for head in range(heads):
        here = slice(head * rows, (head + 1) * rows)
        qs[here, :dim] = q_ref[:, head * dim : (head + 1) * dim]
        qs[here, dim:] = query_marks

    def attend(chunk, first, hooks):
        place = pl.ds(pl.multiple_of(chunk * keys_wide, keys_wide), keys_wide)
        marks = []
        for half in range(2):
            key_col = jnp.broadcast_to(docs[chunk * 2 + half], (dim, rows)).T
            marks.append(jnp.where(lane == key_col, 1.0, 0.0).astype(jnp.bfloat16))
        k_chunk = jnp.concatenate([kv[0, place, :], jnp.concatenate(marks, axis=0)], axis=1)
        v_chunk = jnp.concatenate(
            [kv[1, place, :], jnp.ones((keys_wide, dim), jnp.bfloat16)], axis=1
        )
        if first:
            for part in range(keys_wide // dim):
                key_id = chunk * keys_wide + part * dim + lane
                bias[:, part * dim : (part + 1) * dim] = jnp.where(key_id <= row_id, 0.0, HIDDEN)
        tile_rows = TILE_HEADS * rows

        def scores(tile):
            return lax.dot_general(
                qs[tile * tile_rows : (tile + 1) * tile_rows, :],
                k_chunk,
                (((1,), (1,)), ((), ())),
                preferred_element_type=jnp.float32,
            )

        tiles = heads // TILE_HEADS
        following = scores(0)
        for tile in range(tiles):
            s = following
            if tile + 1 < tiles:
                following = scores(tile + 1)
            here = slice(tile * tile_rows, (tile + 1) * tile_rows)
            if first:
                s = s + jnp.concatenate([bias[...]] * TILE_HEADS, axis=0)
            new = jnp.max(s, axis=1, keepdims=True)
            if first:
                new = jnp.broadcast_to(new, (tile_rows, dim))
            else:
                old = m_ref[here]
                new = jnp.maximum(old, new)
            m_ref[here] = new
            w = jnp.exp2((s - jnp.tile(new, (1, keys_wide // dim))) * scale)
            part = jnp.dot(w.astype(jnp.bfloat16), v_chunk, preferred_element_type=jnp.float32)
            if first:
                acc_ref[here] = part
            else:
                acc_ref[here] = (
                    acc_ref[here] * jnp.tile(jnp.exp2((old - new) * scale), (1, 2)) + part
                )
            if tile < len(hooks):
                hooks[tile]()

    def process(chunk, hooks=()):
        needed = (chunk <= chip) & (chunk * 2 + 1 >= me - window)

        @pl.when(needed)
        def _():
            attend(chunk, False, hooks)

        if hooks:

            @pl.when(jnp.logical_not(needed))
            def _():
                for hook in hooks:
                    hook()

    def from_below(level, piece):
        def hook():
            @pl.when(level > jnp.maximum(z - depth, 0))
            def _():
                arrived(0, level - 1, piece, (level - 1) * 4 + r, up)
                relay(level - 1, piece)

        return hook

    def from_across(level, piece):
        block = level * 4 + 2 * (1 - y) + c

        def hook():
            @pl.when(crossed(level))
            def _():
                arrived(1, level, piece, block, across)
                start(3, level, piece, block, partner)

        return hook

    def own_column(level):
        for piece in range(2):
            arrived(2, level, piece, level * 4 + 2 * y + 1 - c, partner)

    def other_column(level):
        @pl.when(crossed(level))
        def _():
            for piece in range(2):
                arrived(3, level, piece, level * 4 + 2 * (1 - y) + 1 - c, partner)

    def hooks_of(level):
        return (
            from_below(level, 0),
            from_below(level, 1),
            from_across(level, 0),
            from_across(level, 1),
        )

    own_column(z)
    attend(chip, True, hooks_of(z))

    def step(i, carry):
        level = z - i
        own_column(level)
        process(level * 2 + y, hooks_of(level))
        other_column(level + 1)
        process((level + 1) * 2 + 1 - y)
        return carry

    last = jnp.minimum(z, depth)
    lax.fori_loop(1, last + 1, step, 0)
    other_column(z - last)
    process((z - last) * 2 + 1 - y)

    def out_copy(head):
        cols = slice(head * dim, (head + 1) * dim)
        return pltpu.make_async_copy(o_ref.at[:, cols], o_hbm.at[:, cols], out_sem.at[head])

    for head in range(heads):
        here = slice(head * rows, (head + 1) * rows)
        o_ref[:, head * dim : (head + 1) * dim] = (acc_ref[here, :dim] / acc_ref[here, dim:]).astype(
            o_ref.dtype
        )
        out_copy(head).start()

    def finish(i, carry):
        level = z - i
        block = level * 4 + r
        for piece in range(2):

            @pl.when(climbs(level))
            def _():
                sent(0, level, piece, block, up)

            @pl.when(crosses(level))
            def _():
                sent(1, level, piece, block, across)

            sent(2, level, piece, block, partner)

            @pl.when(crossed(level))
            def _():
                sent(3, level, piece, level * 4 + 2 * (1 - y) + c, partner)

        return carry

    lax.fori_loop(0, last + 1, finish, 0)
    for head in range(heads):
        out_copy(head).wait()


def solution(mesh):
    n = mesh.shape["ctx"]

    def on_device(queries, keys, values, doc_ids):
        rows, width = queries.shape
        dim = keys.shape[1]
        heads = width // dim
        levels = n // 4
        anywhere = pl.BlockSpec(memory_space=pl.ANY)
        piece_sems = pltpu.SemaphoreType.DMA((4, levels, 2))
        doc_sems = pltpu.SemaphoreType.DMA((4, levels))
        return pl.pallas_call(
            functools.partial(kernel, n),
            out_shape=jax.ShapeDtypeStruct((rows, width), jnp.bfloat16),
            in_specs=[anywhere] * 4,
            out_specs=anywhere,
            scratch_shapes=[
                pltpu.VMEM((rows, width), jnp.bfloat16),
                pltpu.VMEM((rows, width), jnp.bfloat16),
                pltpu.VMEM((2, n * rows, dim), jnp.bfloat16),
                pltpu.VMEM((n, 1, rows), jnp.int32),
                pltpu.VMEM((rows, 2 * rows), jnp.float32),
                pltpu.VMEM((heads * rows, dim), jnp.float32),
                pltpu.VMEM((heads * rows, 2 * dim), jnp.float32),
                pltpu.VMEM((heads * rows, 2 * dim), jnp.bfloat16),
                pltpu.SemaphoreType.DMA((4,)),
                pltpu.SemaphoreType.DMA((heads,)),
                piece_sems,
                piece_sems,
                doc_sems,
                doc_sems,
            ],
            compiler_params=pltpu.CompilerParams(collective_id=0, has_side_effects=True, vmem_limit_bytes=16 * 1024 * 1024),
        )(*[pltpu.with_memory_space_constraint(a, pltpu.HBM) for a in (queries, keys, values, doc_ids.reshape(1, rows))])

    spec = P(("groups", "ctx"), None)
    return jax.shard_map(
        on_device,
        mesh=mesh,
        in_specs=(spec, spec, spec, P(("groups", "ctx"))),
        out_specs=spec,
        check_vma=False,
    )
```
